32 devices in a mesh: seq: 8 (over y, x, core), tp: 4 (over z).
Axes of the slice: x: 2, y: 2, z: 4, core: 2. Of those that a mesh axis runs over, the one named last changes fastest.
Arguments:
- projected: bfloat16 [1, 8192, 3, 4096], P(None, 'seq', None, 'tp'), may hold values from -6 to 6
- short_kernel: float32 [3, 3, 4096], P(None, None, 'tp'), may hold values from -3 to 3
- filters: float32 [2, 4096, 8192], P(None, ('tp', 'seq')), may hold values from -2 to 2
- skip_gain: float32 [2, 4096], P(None, ('tp', 'seq')), may hold values from -3 to 3
- out_weight: bfloat16 [4096, 4096], P('tp'), may hold values from -0.09375 to 0.09375
- out_grad: bfloat16 [1, 8192, 4096], P(None, 'seq', 'tp'), may hold values from -6 to 6
Outputs:
- output: bfloat16 [1, 8192, 4096], P(None, 'seq', 'tp')
- projected_grad: bfloat16 [1, 8192, 3, 4096], P(None, 'seq', None, 'tp')
- filter_grad: float32 [2, 4096, 8192], P(None, ('tp', 'seq'))
The draws below stay inside these ranges and needn't reach their ends.
All inputs are finite; a program needn't handle non-finite values.
Results may differ from the reference program's by a relative error of at most 0.0095.
Values may be sent and summed in bfloat16 or wider, within the bound.
A program may use at most 384 MiB of HBM per device.

```python
import math
import jax
import jax.numpy as jnp
from jax import lax

D = 4096
LEN = 8192
SEQS = 1
N_TP = 4


def draw_filters(key, part):
    rate_key = jax.random.fold_in(key, 11)
    noise_key = jax.random.fold_in(key, 12)
    rates = jnp.exp(jax.random.uniform(rate_key, (2, D, 1), jnp.float32, math.log(0.5 / LEN), math.log(1.0 / 30.0)))
    positions = jnp.arange(LEN, dtype=jnp.float32)[None, None, :]
    noise = jnp.clip(jax.random.normal(noise_key, (2, D, LEN), jnp.float32), -6.0, 6.0)
    return noise * jnp.sqrt(rates) * jnp.exp(-rates * positions)


def block_scale(rng, extent, pieces, smallest, high):
    loudness, own = 1.0, jax.random.fold_in(rng, 6)
    for position, shards_of in pieces:
        draws = jnp.exp(jax.random.uniform(jax.random.fold_in(own, position), (shards_of,), jnp.float32, smallest / len(pieces), high / len(pieces)))
        loudness = loudness * jnp.repeat(draws, extent[position] // shards_of).reshape([-1 if axis == position else 1 for axis in range(len(extent))])
    return loudness


def gaussian(stream_key, extent, spread, limit, split=(), kind=jnp.bfloat16):
    drawn = jax.random.normal(stream_key, extent, jnp.float32) * spread
    if len(split) > 0:
        drawn = block_scale(stream_key, extent, split, -0.22, 0.18) * drawn
    return jnp.clip(drawn, min=-limit, max=limit).astype(kind)


def setup_inputs(seed: int = 0) -> dict:
    streams_of = jax.random.split(jax.random.key(seed), 7)
    return {
        "projected": gaussian(streams_of[0], (SEQS, LEN, 3, D), 1.0, 6.0, ((1, 8), (3, 4))),
        "short_kernel": gaussian(streams_of[1], (3, 3, D), 0.6, 3.0, ((2, 4),), jnp.float32),
        "filters": draw_filters(jax.random.fold_in(streams_of[6], 71), 0),
        "skip_gain": gaussian(streams_of[3], (2, D), 1.0, 3.0, ((1, 32),), jnp.float32),
        "out_weight": gaussian(streams_of[4], (D, D), D ** -0.5, 0.09375, ((0, 4),)),
        "out_grad": gaussian(streams_of[5], (SEQS, LEN, D), 1.0, 6.0, ((1, 8), (2, 4))),
    }


def causal_conv(signal, filter_spectrum, length):
    spectrum = jnp.fft.rfft(signal, n=2 * length, axis=-1)
    return jnp.fft.irfft(spectrum * filter_spectrum, n=2 * length, axis=-1)[..., :length]


def correlate(left_spectrum, right_spectrum, length):
    return jnp.fft.irfft(jnp.conj(left_spectrum) * right_spectrum, n=2 * length, axis=-1)[..., :length]


def forward_block(package):
    short_block, filt, gain = package
    short_v = short_block[0].astype(jnp.float32)
    short_x1 = short_block[1].astype(jnp.float32)
    spec_zero = jnp.fft.rfft(filt[0], n=2 * LEN, axis=-1)
    spec_one = jnp.fft.rfft(filt[1], n=2 * LEN, axis=-1)
    first_conv = gain[0][None, :, None] * short_v + causal_conv(short_v, spec_zero[None], LEN)
    middle = short_x1 * first_conv
    second = gain[1][None, :, None] * middle + causal_conv(middle, spec_one[None], LEN)
    return second.astype(jnp.bfloat16)


def backward_block(package):
    short_block, filt, gain, back_second = package
    short_v = short_block[0].astype(jnp.float32)
    short_x1 = short_block[1].astype(jnp.float32)
    spec_zero = jnp.fft.rfft(filt[0], n=2 * LEN, axis=-1)
    spec_one = jnp.fft.rfft(filt[1], n=2 * LEN, axis=-1)
    spec_short = jnp.fft.rfft(short_v, n=2 * LEN, axis=-1)
    first_conv = gain[0][None, :, None] * short_v + jnp.fft.irfft(spec_short * spec_zero[None], n=2 * LEN, axis=-1)[..., :LEN]
    middle = short_x1 * first_conv
    spec_middle = jnp.fft.rfft(middle, n=2 * LEN, axis=-1)
    back_sec = back_second.astype(jnp.float32)
    spec_back_sec = jnp.fft.rfft(back_sec, n=2 * LEN, axis=-1)
    back_middle = gain[1][None, :, None] * back_sec + correlate(spec_one[None], spec_back_sec, LEN)
    grad_one = jnp.sum(correlate(spec_middle, spec_back_sec, LEN), axis=0)
    back_x1 = (back_middle * first_conv).astype(jnp.bfloat16)
    back_first = back_middle * short_x1
    spec_back_first = jnp.fft.rfft(back_first, n=2 * LEN, axis=-1)
    back_v = (gain[0][None, :, None] * back_first + correlate(spec_zero[None], spec_back_first, LEN)).astype(jnp.bfloat16)
    grad_zero = jnp.sum(correlate(spec_short, spec_back_first, LEN), axis=0)
    return back_v, back_x1, jnp.stack([grad_zero, grad_one])


def reference(projected, short_kernel, filters, skip_gain, out_weight, out_grad):
    seq_count, length, _, width = projected.shape
    chan_block = math.gcd(width, 256)
    block_count = width // chan_block
    padded = jnp.pad(projected.astype(jnp.float32), ((0, 0), (2, 0), (0, 0), (0, 0)))
    short = sum(short_kernel[:, offset, :] * padded[:, 2 - offset:2 - offset + length] for offset in range(3)).astype(jnp.bfloat16)
    channel = jnp.transpose(short, (2, 0, 3, 1)).reshape(3, seq_count, block_count, chan_block, length).transpose(2, 0, 1, 3, 4)
    filt_blocks = filters.reshape(2, block_count, chan_block, length).transpose(1, 0, 2, 3)
    gain_blocks = skip_gain.reshape(2, block_count, chan_block).transpose(1, 0, 2)

    def unblock(blocked):
        return blocked.transpose(1, 0, 2, 3).reshape(seq_count, width, length).transpose(0, 2, 1)

    second = unblock(lax.map(forward_block, (channel, filt_blocks, gain_blocks)))
    short_x2 = short[:, :, 2, :].astype(jnp.float32)
    gated = (short_x2 * second.astype(jnp.float32)).astype(jnp.bfloat16)
    flat_gated = gated.reshape(seq_count * length, width)
    group = width // N_TP
    output = jnp.zeros((seq_count * length, width), jnp.float32)
    for member in range(N_TP):
        partial_out = jnp.dot(flat_gated[:, member * group:(member + 1) * group], out_weight[member * group:(member + 1) * group], preferred_element_type=jnp.float32)
        output = output + partial_out.astype(jnp.bfloat16).astype(jnp.float32)
    output = output.astype(jnp.bfloat16).reshape(seq_count, length, width)
    back_gated = lax.dot_general(out_grad.reshape(seq_count * length, width), out_weight, (((1,), (1,)), ((), ())), preferred_element_type=jnp.float32)
    back_gated = back_gated.astype(jnp.bfloat16).reshape(seq_count, length, width).astype(jnp.float32)
    back_second = (back_gated * short_x2).astype(jnp.bfloat16)
    back_x2 = (back_gated * second.astype(jnp.float32)).astype(jnp.bfloat16)
    back_blocks = back_second.transpose(0, 2, 1).reshape(seq_count, block_count, chan_block, length).transpose(1, 0, 2, 3)
    back_v, back_x1, grad_blocks = lax.map(backward_block, (channel, filt_blocks, gain_blocks, back_blocks))
    back_all = jnp.stack([unblock(back_v), unblock(back_x1), back_x2], axis=2)
    tail = jnp.pad(back_all.astype(jnp.float32), ((0, 0), (0, 2), (0, 0), (0, 0)))
    projected_grad = sum(short_kernel[:, offset, :] * tail[:, offset:offset + length] for offset in range(3)).astype(jnp.bfloat16)
    filter_grad = grad_blocks.transpose(1, 0, 2, 3).reshape(2, width, length) * (seq_count * length) ** -0.5
    return output, projected_grad, filter_grad
```

```python
import functools
import math

import jax
import jax.numpy as jnp
import numpy as np
from jax import lax
from jax.experimental import pallas as pl
from jax.experimental.pallas import tpu as pltpu
from jax.sharding import PartitionSpec as P

F32 = jnp.float32
BF16 = jnp.bfloat16
INNER = 128
SUB = 8
ROWS = 16
SIDE = 4


def small_tables(outer):
    total = outer * INNER
    twist = 2.0 * math.pi * (np.arange(outer)[:, None] + 0.25) * np.arange(INNER)[None, :] / total
    ids = np.arange(INNER)
    inner = 2.0 * math.pi * (ids[:, None] * ids[None, :] % INNER) / INNER
    parts = [np.cos(twist), np.sin(twist), np.cos(inner), np.sin(inner)]
    return [jnp.asarray(p, F32) for p in parts] + [jnp.zeros((), jnp.int32)]


def spread_table(outer, freq_dim, start, scale):
    shape = [outer * SUB, outer * SUB]
    shape[freq_dim] *= 2
    freq = lax.broadcasted_iota(jnp.int32, shape, freq_dim) + start
    time = lax.broadcasted_iota(jnp.int32, shape, 1 - freq_dim)
    row = freq // SUB
    turn = 4 * outer
    phase = (4 * (row % outer) + 1) * (time // SUB) + outer * (row // outer)
    value = jnp.cos((phase % turn).astype(F32) * (2.0 * math.pi / turn)) * scale
    return jnp.where(freq % SUB == time % SUB, value, 0.0).astype(BF16)


def transform_tables(outer):
    tc, ts, ic, is_, start = lax.optimization_barrier(tuple(small_tables(outer)))
    opening = spread_table(outer, 0, start, 1.0)
    closing = spread_table(outer, 1, start, 1.0 / (outer * INNER))
    cos = tc[:, None, :] * ic[None] - ts[:, None, :] * is_[None]
    sin = ts[:, None, :] * ic[None] + tc[:, None, :] * is_[None]
    mix = jnp.concatenate(
        [jnp.concatenate([cos, sin], axis=2), jnp.concatenate([-sin, cos], axis=2)], axis=1
    ).astype(BF16)
    cos_t = tc[:, :, None] * ic[None] - ts[:, :, None] * is_[None]
    sin_t = ts[:, :, None] * ic[None] + tc[:, :, None] * is_[None]
    unmix = jnp.concatenate(
        [jnp.concatenate([cos_t, -sin_t], axis=2), jnp.concatenate([sin_t, cos_t], axis=2)], axis=1
    ).astype(BF16)
    return opening, closing, mix, unmix


def mul(a, b):
    return jnp.dot(a, b, preferred_element_type=F32)


def open_rows(opening, signal):
    outer, rows, lanes = signal.shape
    wide = jnp.concatenate([signal[:, at : at + SUB] for at in range(0, rows, SUB)], axis=2)
    flat = wide.reshape(outer * SUB, wide.shape[2]).astype(BF16)
    out = mul(opening, flat).reshape(2 * outer, SUB, wide.shape[2])
    parts = [out[:, :, at : at + lanes] for at in range(0, wide.shape[2], lanes)]
    return jnp.concatenate(parts, axis=1).astype(BF16)


def close_rows(closing, mixed):
    twice, rows, lanes = mixed.shape
    full = mixed.astype(F32)
    wide = jnp.concatenate([full[:, at : at + SUB] for at in range(0, rows, SUB)], axis=2)
    flat = wide.reshape(twice * SUB, wide.shape[2]).astype(BF16)
    out = mul(closing, flat).reshape(twice // 2, SUB, wide.shape[2])
    parts = [out[:, :, at : at + lanes] for at in range(0, wide.shape[2], lanes)]
    return jnp.concatenate(parts, axis=1)


def open_filters_body(opening, filt, out0, out1):
    out0[...] = open_rows(opening[...], filt[0])
    out1[...] = open_rows(opening[...], filt[1])


def open_v_body(opening, v, out):
    out[...] = open_rows(opening[...], v[...].astype(F32))


def open_back_body(opening, x2, bg, second, out, bx2):
    bgv = bg[...].astype(F32)
    bs = (bgv * x2[...].astype(F32)).astype(BF16).astype(F32)
    bx2[...] = (bgv * second[...].astype(F32)).astype(BF16)
    out[...] = open_rows(opening[...], bs)


def halves(spec):
    return spec[:INNER], spec[INNER:]


def cmul(a, b):
    (ar, ai), (br, bi) = a, b
    return ar * br - ai * bi, ar * bi + ai * br


def conj_mul(a, b):
    (ar, ai), (br, bi) = a, b
    return ar * br + ai * bi, ar * bi - ai * br


def lane_halves(spec):
    width = spec.shape[1] // 2
    re, im = halves(spec)
    return (re[:, :width], im[:, :width]), (re[:, width:], im[:, width:])


def joined(left, right):
    re = jnp.concatenate([left[0], right[0]], axis=1)
    im = jnp.concatenate([left[1], right[1]], axis=1)
    return jnp.concatenate([re, im], axis=0).astype(BF16)


def column(ref, i):
    return jnp.concatenate([ref[0, i], ref[1, i]], axis=0)


def put_column(ref, i, value):
    value = value.astype(BF16)
    ref[0, i] = value[:INNER]
    ref[1, i] = value[INNER:]


def pair_spec(table, left, right, i):
    both = jnp.concatenate([column(left, i), column(right, i)], axis=1)
    return lane_halves(mul(table, both))


def conv_body(mix, unmix, filt, sig, out):
    for i in range(SIDE):
        f, x = pair_spec(mix[i], filt, sig, i)
        re, im = cmul(x, f)
        put_column(out, i, mul(unmix[i], jnp.concatenate([re, im], axis=0).astype(BF16)))


def correlate_body(mix, unmix, filt, sig, later, out, grads):
    for i in range(SIDE):
        f, back = pair_spec(mix[i], filt, later, i)
        x = halves(mul(mix[i], column(sig, i)))
        both = mul(unmix[i], joined(conj_mul(f, back), conj_mul(x, back)))
        width = both.shape[1] // 2
        put_column(out, i, both[:, :width])
        put_column(grads, i, both[:, width:])


def turn_body(opening, closing, gain, mixed, v, x1, out, first_out, mid_out):
    g0 = gain[0:1, :][None]
    first = g0 * v[...].astype(F32) + close_rows(closing[...], mixed[...])
    mid = x1[...].astype(F32) * first
    first_out[...] = first
    mid_out[...] = mid
    out[...] = open_rows(opening[...], mid)


def second_body(closing, gain, mixed, mid, x2, second_out, gated):
    g1 = gain[1:2, :][None]
    second = (g1 * mid[...] + close_rows(closing[...], mixed[...])).astype(BF16)
    second_out[...] = second
    gated[...] = (x2[...].astype(F32) * second.astype(F32)).astype(BF16)


def turn_back_body(scale, opening, closing, gain, mixed, grads, x1, x2, bg, first, out, bf_out, bx1, grad):
    g1 = gain[1:2, :][None]
    bs = (bg[...].astype(F32) * x2[...].astype(F32)).astype(BF16).astype(F32)
    back_middle = g1 * bs + close_rows(closing[...], mixed[...])
    bf = back_middle * x1[...].astype(F32)
    bf_out[...] = bf
    bx1[...] = (back_middle * first[...]).astype(BF16)
    out[...] = open_rows(opening[...], bf)
    grad[...] = close_rows(closing[...], grads[...]) * scale


def finish_body(scale, closing, gain, mixed, grads, bf, bv, grad):
    g0 = gain[0:1, :][None]
    bv[...] = (g0 * bf[...] + close_rows(closing[...], mixed[...])).astype(BF16)
    grad[...] = close_rows(closing[...], grads[...]) * scale


def whole(array):
    return pl.BlockSpec(array.shape, lambda i: (0,) * array.ndim)


def rows_spec(lead, lanes):
    return pl.BlockSpec((lead, ROWS, lanes), lambda i: (0, i, 0))


def side_spec(lanes):
    return pl.BlockSpec((2, SIDE, INNER, lanes), lambda i: (0, i, 0, 0))


params = pltpu.CompilerParams(vmem_limit_bytes=56 << 20)


def rows_pass(name, body, wholes, blocks, outs):
    inner, width = blocks[0].shape[-2:]
    specs = []
    for block in blocks:
        if block.ndim == 4:
            specs.append(pl.BlockSpec(block.shape[:2] + (ROWS, width), lambda i: (0, 0, i, 0)))
        else:
            specs.append(rows_spec(block.shape[0], width))
    return pl.pallas_call(
        body,
        grid=(inner // ROWS,),
        in_specs=[whole(w) for w in wholes] + specs,
        out_specs=[rows_spec(lead, width) for lead, _ in outs],
        out_shape=[jax.ShapeDtypeStruct((lead, inner, width), kind) for lead, kind in outs],
        compiler_params=params,
        name=name,
    )(*wholes, *blocks)


def middle_pass(name, body, count, tables, *columns):
    _, _, mix, unmix = tables
    outer = mix.shape[0]
    _, inner, lanes = columns[0].shape
    columns = [c.reshape(2, outer, inner, lanes) for c in columns]
    table_spec = pl.BlockSpec((SIDE,) + mix.shape[1:], lambda i: (i, 0, 0))
    out = pl.pallas_call(
        body,
        grid=(outer // SIDE,),
        in_specs=[table_spec, table_spec] + [side_spec(lanes)] * len(columns),
        out_specs=[side_spec(lanes)] * count,
        out_shape=[jax.ShapeDtypeStruct(columns[0].shape, BF16)] * count,
        compiler_params=params,
        name=name,
    )(mix, unmix, *columns)
    return [o.reshape(2 * outer, inner, lanes) for o in out]


def forward_core(tables, gain, filters, v, x1, x2):
    opening, closing, _, _ = tables
    outer = v.shape[0]
    twice = 2 * outer
    filt = jnp.swapaxes(filters, 1, 2).reshape((2,) + v.shape)
    f0, f1 = rows_pass(
        "open_filters", open_filters_body, [opening], [filt], [(twice, BF16), (twice, BF16)]
    )
    (sv,) = rows_pass("open_v", open_v_body, [opening], [v], [(twice, BF16)])
    (mixed,) = middle_pass("conv_first", conv_body, 1, tables, f0, sv)
    sm, first, mid = rows_pass(
        "turn",
        turn_body,
        [opening, closing, gain],
        [mixed, v, x1],
        [(twice, BF16), (outer, F32), (outer, F32)],
    )
    (mixed,) = middle_pass("conv_second", conv_body, 1, tables, f1, sm)
    second, gated = rows_pass(
        "second", second_body, [closing, gain], [mixed, mid, x2], [(outer, BF16), (outer, BF16)]
    )
    return f0, f1, sv, sm, first, second, gated


def backward_core(tables, gain, kept, x1, x2, bg):
    opening, closing, _, _ = tables
    f0, f1, sv, sm, first, second, _ = kept
    outer, inner, _ = x1.shape
    twice = 2 * outer
    scale = float(outer * inner) ** -0.5
    sb, bx2 = rows_pass(
        "open_back", open_back_body, [opening], [x2, bg, second], [(twice, BF16), (outer, BF16)]
    )
    mixed, grads = middle_pass("corr_second", correlate_body, 2, tables, f1, sm, sb)
    sf, bf, bx1, grad1 = rows_pass(
        "turn_back",
        functools.partial(turn_back_body, scale),
        [opening, closing, gain],
        [mixed, grads, x1, x2, bg, first],
        [(twice, BF16), (outer, F32), (outer, BF16), (outer, F32)],
    )
    mixed, grads = middle_pass("corr_first", correlate_body, 2, tables, f0, sv, sf)
    bv, grad0 = rows_pass(
        "finish",
        functools.partial(finish_body, scale),
        [closing, gain],
        [mixed, grads, bf],
        [(outer, BF16), (outer, F32)],
    )
    turned = [jnp.transpose(g.reshape(outer * inner, -1)) for g in (grad0, grad1)]
    return bv, bx1, bx2, jnp.stack(turned)


def core(tables, gain, filters, v, x1, x2, bg):
    kept = forward_core(tables, gain, filters, v, x1, x2)
    bv, bx1, bx2, grad = backward_core(tables, gain, kept, x1, x2, bg)
    return kept[-1], bx1, bx2, bv, grad


def to_channels(block):
    count = lax.axis_size("seq")
    frames, local_width = block.shape
    split = jnp.swapaxes(block.reshape(frames, count, local_width // count), 0, 1)
    moved = lax.all_to_all(split, "seq", split_axis=0, concat_axis=0, tiled=True)
    return moved.reshape(count * frames, local_width // count)


def to_frames(block):
    count = lax.axis_size("seq")
    length, width = block.shape
    return lax.all_to_all(
        block.reshape(count, length // count, width), "seq", split_axis=0, concat_axis=0, tiled=True
    )


def short_filter(block, taps):
    wide = jnp.pad(block.astype(F32), ((2, 0), (0, 0)))
    length = block.shape[0]
    return sum(taps[j][None] * wide[2 - j : 2 - j + length] for j in range(3)).astype(BF16)


def short_filter_back(block, taps):
    wide = jnp.pad(block.astype(F32), ((0, 2), (0, 0)))
    length = block.shape[0]
    return sum(taps[j][None] * wide[j : j + length] for j in range(3)).astype(BF16)


def local(projected, short_kernel, filters, skip_gain, out_weight, out_grad):
    _, frames, _, local_width = projected.shape
    _, width, length = filters.shape
    outer = length // INNER
    grid3 = (outer, INNER, width)
    mine = lax.axis_index("seq") * width
    taps = lax.dynamic_slice_in_dim(short_kernel, mine, width, axis=2)
    tables = transform_tables(outer)

    raw = [to_channels(projected[0, :, s]) for s in range(3)]
    back_gated = lax.dot_general(
        lax.all_gather(out_grad[0], "tp", axis=1, tiled=True),
        out_weight,
        (((1,), (1,)), ((), ())),
        preferred_element_type=F32,
    ).astype(BF16)
    bg = to_channels(back_gated).reshape(grid3)

    v, x1, x2 = [short_filter(raw[s], taps[s]).reshape(grid3) for s in range(3)]
    kept = forward_core(tables, skip_gain, filters, v, x1, x2)
    gated = kept[-1]
    bv, bx1, bx2, filter_grad = backward_core(tables, skip_gain, kept, x1, x2, bg)

    flat_gated = jnp.swapaxes(to_frames(gated.reshape(length, width)), 0, 1)
    flat_gated = flat_gated.reshape(frames, local_width)
    summed = lax.psum_scatter(
        lax.dot_general(
            out_weight, flat_gated, (((0,), (1,)), ((), ())), preferred_element_type=F32
        ).astype(BF16),
        "tp",
        scatter_dimension=0,
        tiled=True,
    )
    output = jnp.transpose(summed)[None]

    moved = [
        to_frames(short_filter_back(b.reshape(length, width), taps[s]))
        for s, b in ((1, bx1), (0, bv), (2, bx2))
    ]
    stacked = jnp.stack([moved[1], moved[0], moved[2]])
    projected_grad = jnp.transpose(stacked, (2, 0, 1, 3)).reshape(1, frames, 3, local_width)
    return (output, projected_grad, filter_grad)


def solution(mesh):
    in_specs = (
        P(None, "seq", None, "tp"),
        P(None, None, "tp"),
        P(None, ("tp", "seq"), None),
        P(None, ("tp", "seq")),
        P("tp", None),
        P(None, "seq", "tp"),
    )
    out_specs = (P(None, "seq", "tp"), P(None, "seq", None, "tp"), P(None, ("tp", "seq"), None))
    return jax.shard_map(local, mesh=mesh, in_specs=in_specs, out_specs=out_specs, check_vma=False)
```

```python
import functools
import math

import jax
import jax.numpy as jnp
import numpy as np
from jax import lax
from jax.experimental import pallas as pl
from jax.experimental.pallas import tpu as pltpu
from jax.sharding import PartitionSpec as P

F32 = jnp.float32
BF16 = jnp.bfloat16
INNER = 128
SUB = 8
ROWS = 16
SIDE = 8


def small_tables(outer):
    total = outer * INNER
    twist = 2.0 * math.pi * (np.arange(outer)[:, None] + 0.25) * np.arange(INNER)[None, :] / total
    ids = np.arange(INNER)
    inner = 2.0 * math.pi * (ids[:, None] * ids[None, :] % INNER) / INNER
    parts = [np.cos(twist), np.sin(twist), np.cos(inner), np.sin(inner)]
    return [jnp.asarray(p, F32) for p in parts] + [jnp.zeros((), jnp.int32)]


def spread_table(outer, freq_dim, start, scale):
    shape = [outer * SUB, outer * SUB]
    shape[freq_dim] *= 2
    freq = lax.broadcasted_iota(jnp.int32, shape, freq_dim) + start
    time = lax.broadcasted_iota(jnp.int32, shape, 1 - freq_dim)
    row = freq // SUB
    turn = 4 * outer
    phase = (4 * (row % outer) + 1) * (time // SUB) + outer * (row // outer)
    value = jnp.cos((phase % turn).astype(F32) * (2.0 * math.pi / turn)) * scale
    return jnp.where(freq % SUB == time % SUB, value, 0.0).astype(BF16)


def transform_tables(outer):
    tc, ts, ic, is_, start = lax.optimization_barrier(tuple(small_tables(outer)))
    opening = spread_table(outer, 0, start, 1.0)
    closing = spread_table(outer, 1, start, 1.0 / (outer * INNER))
    cos = tc[:, None, :] * ic[None] - ts[:, None, :] * is_[None]
    sin = ts[:, None, :] * ic[None] + tc[:, None, :] * is_[None]
    mix = jnp.concatenate(
        [jnp.concatenate([cos, sin], axis=2), jnp.concatenate([-sin, cos], axis=2)], axis=1
    ).astype(BF16)
    cos_t = tc[:, :, None] * ic[None] - ts[:, :, None] * is_[None]
    sin_t = ts[:, :, None] * ic[None] + tc[:, :, None] * is_[None]
    unmix = jnp.concatenate(
        [jnp.concatenate([cos_t, -sin_t], axis=2), jnp.concatenate([sin_t, cos_t], axis=2)], axis=1
    ).astype(BF16)
    return opening, closing, mix, unmix


def mul(a, b):
    return jnp.dot(a, b, preferred_element_type=F32)


def open_rows(opening, signal):
    outer, rows, lanes = signal.shape
    wide = jnp.concatenate([signal[:, at : at + SUB] for at in range(0, rows, SUB)], axis=2)
    flat = wide.reshape(outer * SUB, wide.shape[2]).astype(BF16)
    out = mul(opening, flat).reshape(2 * outer, SUB, wide.shape[2])
    parts = [out[:, :, at : at + lanes] for at in range(0, wide.shape[2], lanes)]
    return jnp.concatenate(parts, axis=1).astype(BF16)


def close_rows(closing, mixed):
    twice, rows, lanes = mixed.shape
    full = mixed.astype(F32)
    wide = jnp.concatenate([full[:, at : at + SUB] for at in range(0, rows, SUB)], axis=2)
    flat = wide.reshape(twice * SUB, wide.shape[2]).astype(BF16)
    out = mul(closing, flat).reshape(twice // 2, SUB, wide.shape[2])
    parts = [out[:, :, at : at + lanes] for at in range(0, wide.shape[2], lanes)]
    return jnp.concatenate(parts, axis=1)


def open_filters_body(opening, filt, out0, out1):
    out0[...] = open_rows(opening[...], filt[0])
    out1[...] = open_rows(opening[...], filt[1])


def open_v_body(opening, v, out):
    out[...] = open_rows(opening[...], v[...].astype(F32))


def open_back_body(opening, x2, bg, second, out, bx2):
    bgv = bg[...].astype(F32)
    bs = (bgv * x2[...].astype(F32)).astype(BF16).astype(F32)
    bx2[...] = (bgv * second[...].astype(F32)).astype(BF16)
    out[...] = open_rows(opening[...], bs)


def halves(spec):
    return spec[:INNER], spec[INNER:]


def cmul(a, b):
    (ar, ai), (br, bi) = a, b
    return ar * br - ai * bi, ar * bi + ai * br


def conj_mul(a, b):
    (ar, ai), (br, bi) = a, b
    return ar * br + ai * bi, ar * bi - ai * br


def lane_halves(spec):
    width = spec.shape[1] // 2
    re, im = halves(spec)
    return (re[:, :width], im[:, :width]), (re[:, width:], im[:, width:])


def joined(left, right):
    re = jnp.concatenate([left[0], right[0]], axis=1)
    im = jnp.concatenate([left[1], right[1]], axis=1)
    return jnp.concatenate([re, im], axis=0).astype(BF16)


def column(ref, i):
    return jnp.concatenate([ref[0, i], ref[1, i]], axis=0)


def put_column(ref, i, value):
    value = value.astype(BF16)
    ref[0, i] = value[:INNER]
    ref[1, i] = value[INNER:]


def pair_spec(table, left, right, i):
    both = jnp.concatenate([column(left, i), column(right, i)], axis=1)
    return lane_halves(mul(table, both))


def conv_body(mix, unmix, filt, sig, out):
    for i in range(SIDE):
        f, x = pair_spec(mix[i], filt, sig, i)
        re, im = cmul(x, f)
        put_column(out, i, mul(unmix[i], jnp.concatenate([re, im], axis=0).astype(BF16)))


def correlate_body(mix, unmix, filt, sig, later, out, grads):
    for i in range(SIDE):
        f, back = pair_spec(mix[i], filt, later, i)
        x = halves(mul(mix[i], column(sig, i)))
        both = mul(unmix[i], joined(conj_mul(f, back), conj_mul(x, back)))
        width = both.shape[1] // 2
        put_column(out, i, both[:, :width])
        put_column(grads, i, both[:, width:])


def turn_body(opening, closing, gain, mixed, v, x1, out, first_out, mid_out):
    g0 = gain[0:1, :][None]
    first = g0 * v[...].astype(F32) + close_rows(closing[...], mixed[...])
    mid = x1[...].astype(F32) * first
    first_out[...] = first
    mid_out[...] = mid
    out[...] = open_rows(opening[...], mid)


def second_body(closing, gain, mixed, mid, x2, second_out, gated):
    g1 = gain[1:2, :][None]
    second = (g1 * mid[...] + close_rows(closing[...], mixed[...])).astype(BF16)
    second_out[...] = second
    gated[...] = (x2[...].astype(F32) * second.astype(F32)).astype(BF16)


def turn_back_body(scale, opening, closing, gain, mixed, grads, x1, x2, bg, first, out, bf_out, bx1, grad):
    g1 = gain[1:2, :][None]
    bs = (bg[...].astype(F32) * x2[...].astype(F32)).astype(BF16).astype(F32)
    back_middle = g1 * bs + close_rows(closing[...], mixed[...])
    bf = back_middle * x1[...].astype(F32)
    bf_out[...] = bf
    bx1[...] = (back_middle * first[...]).astype(BF16)
    out[...] = open_rows(opening[...], bf)
    grad[...] = close_rows(closing[...], grads[...]) * scale


def finish_body(scale, closing, gain, mixed, grads, bf, bv, grad):
    g0 = gain[0:1, :][None]
    bv[...] = (g0 * bf[...] + close_rows(closing[...], mixed[...])).astype(BF16)
    grad[...] = close_rows(closing[...], grads[...]) * scale


def whole(array):
    return pl.BlockSpec(array.shape, lambda i: (0,) * array.ndim)


def rows_spec(lead, lanes):
    return pl.BlockSpec((lead, ROWS, lanes), lambda i: (0, i, 0))


def side_spec(lanes):
    return pl.BlockSpec((2, SIDE, INNER, lanes), lambda i: (0, i, 0, 0))


params = pltpu.CompilerParams(vmem_limit_bytes=56 << 20)


def rows_pass(name, body, wholes, blocks, outs):
    inner, width = blocks[0].shape[-2:]
    specs = []
    for block in blocks:
        if block.ndim == 4:
            specs.append(pl.BlockSpec(block.shape[:2] + (ROWS, width), lambda i: (0, 0, i, 0)))
        else:
            specs.append(rows_spec(block.shape[0], width))
    return pl.pallas_call(
        body,
        grid=(inner // ROWS,),
        in_specs=[whole(w) for w in wholes] + specs,
        out_specs=[rows_spec(lead, width) for lead, _ in outs],
        out_shape=[jax.ShapeDtypeStruct((lead, inner, width), kind) for lead, kind in outs],
        compiler_params=params,
        name=name,
    )(*wholes, *blocks)


def middle_pass(name, body, count, tables, *columns):
    _, _, mix, unmix = tables
    outer = mix.shape[0]
    _, inner, lanes = columns[0].shape
    columns = [c.reshape(2, outer, inner, lanes) for c in columns]
    table_spec = pl.BlockSpec((SIDE,) + mix.shape[1:], lambda i: (i, 0, 0))
    out = pl.pallas_call(
        body,
        grid=(outer // SIDE,),
        in_specs=[table_spec, table_spec] + [side_spec(lanes)] * len(columns),
        out_specs=[side_spec(lanes)] * count,
        out_shape=[jax.ShapeDtypeStruct(columns[0].shape, BF16)] * count,
        compiler_params=params,
        name=name,
    )(mix, unmix, *columns)
    return [o.reshape(2 * outer, inner, lanes) for o in out]


def forward_core(tables, gain, filters, v, x1, x2):
    opening, closing, _, _ = tables
    outer = v.shape[0]
    twice = 2 * outer
    filt = jnp.swapaxes(filters, 1, 2).reshape((2,) + v.shape)
    f0, f1 = rows_pass(
        "open_filters", open_filters_body, [opening], [filt], [(twice, BF16), (twice, BF16)]
    )
    (sv,) = rows_pass("open_v", open_v_body, [opening], [v], [(twice, BF16)])
    (mixed,) = middle_pass("conv_first", conv_body, 1, tables, f0, sv)
    sm, first, mid = rows_pass(
        "turn",
        turn_body,
        [opening, closing, gain],
        [mixed, v, x1],
        [(twice, BF16), (outer, F32), (outer, F32)],
    )
    (mixed,) = middle_pass("conv_second", conv_body, 1, tables, f1, sm)
    second, gated = rows_pass(
        "second", second_body, [closing, gain], [mixed, mid, x2], [(outer, BF16), (outer, BF16)]
    )
    return f0, f1, sv, sm, first, second, gated


def backward_core(tables, gain, kept, x1, x2, bg):
    opening, closing, _, _ = tables
    f0, f1, sv, sm, first, second, _ = kept
    outer, inner, _ = x1.shape
    twice = 2 * outer
    scale = float(outer * inner) ** -0.5
    sb, bx2 = rows_pass(
        "open_back", open_back_body, [opening], [x2, bg, second], [(twice, BF16), (outer, BF16)]
    )
    mixed, grads = middle_pass("corr_second", correlate_body, 2, tables, f1, sm, sb)
    sf, bf, bx1, grad1 = rows_pass(
        "turn_back",
        functools.partial(turn_back_body, scale),
        [opening, closing, gain],
        [mixed, grads, x1, x2, bg, first],
        [(twice, BF16), (outer, F32), (outer, BF16), (outer, F32)],
    )
    mixed, grads = middle_pass("corr_first", correlate_body, 2, tables, f0, sv, sf)
    bv, grad0 = rows_pass(
        "finish",
        functools.partial(finish_body, scale),
        [closing, gain],
        [mixed, grads, bf],
        [(outer, BF16), (outer, F32)],
    )
    turned = [jnp.transpose(g.reshape(outer * inner, -1)) for g in (grad0, grad1)]
    return bv, bx1, bx2, jnp.stack(turned)


def core(tables, gain, filters, v, x1, x2, bg):
    kept = forward_core(tables, gain, filters, v, x1, x2)
    bv, bx1, bx2, grad = backward_core(tables, gain, kept, x1, x2, bg)
    return kept[-1], bx1, bx2, bv, grad


def to_channels(block):
    count = lax.axis_size("seq")
    frames, local_width = block.shape
    split = jnp.swapaxes(block.reshape(frames, count, local_width // count), 0, 1)
    moved = lax.all_to_all(split, "seq", split_axis=0, concat_axis=0, tiled=True)
    return moved.reshape(count * frames, local_width // count)


def to_frames(block):
    count = lax.axis_size("seq")
    length, width = block.shape
    return lax.all_to_all(
        block.reshape(count, length // count, width), "seq", split_axis=0, concat_axis=0, tiled=True
    )


def short_filter(block, taps):
    wide = jnp.pad(block.astype(F32), ((2, 0), (0, 0)))
    length = block.shape[0]
    return sum(taps[j][None] * wide[2 - j : 2 - j + length] for j in range(3)).astype(BF16)


def short_filter_back(block, taps):
    wide = jnp.pad(block.astype(F32), ((0, 2), (0, 0)))
    length = block.shape[0]
    return sum(taps[j][None] * wide[j : j + length] for j in range(3)).astype(BF16)


def local(projected, short_kernel, filters, skip_gain, out_weight, out_grad):
    _, frames, _, local_width = projected.shape
    _, width, length = filters.shape
    outer = length // INNER
    grid3 = (outer, INNER, width)
    mine = lax.axis_index("seq") * width
    taps = lax.dynamic_slice_in_dim(short_kernel, mine, width, axis=2)
    tables = transform_tables(outer)

    raw = [to_channels(projected[0, :, s]) for s in range(3)]
    back_gated = lax.dot_general(
        lax.all_gather(out_grad[0], "tp", axis=1, tiled=True),
        out_weight,
        (((1,), (1,)), ((), ())),
        preferred_element_type=F32,
    ).astype(BF16)
    bg = to_channels(back_gated).reshape(grid3)

    v, x1, x2 = [short_filter(raw[s], taps[s]).reshape(grid3) for s in range(3)]
    kept = forward_core(tables, skip_gain, filters, v, x1, x2)
    gated = kept[-1]
    bv, bx1, bx2, filter_grad = backward_core(tables, skip_gain, kept, x1, x2, bg)

    flat_gated = jnp.swapaxes(to_frames(gated.reshape(length, width)), 0, 1)
    flat_gated = flat_gated.reshape(frames, local_width)
    summed = lax.psum_scatter(
        lax.dot_general(
            out_weight, flat_gated, (((0,), (1,)), ((), ())), preferred_element_type=F32
        ).astype(BF16),
        "tp",
        scatter_dimension=0,
        tiled=True,
    )
    output = jnp.transpose(summed)[None]

    moved = [
        to_frames(short_filter_back(b.reshape(length, width), taps[s]))
        for s, b in ((1, bx1), (0, bv), (2, bx2))
    ]
    stacked = jnp.stack([moved[1], moved[0], moved[2]])
    projected_grad = jnp.transpose(stacked, (2, 0, 1, 3)).reshape(1, frames, 3, local_width)
    return (output, projected_grad, filter_grad)


def solution(mesh):
    in_specs = (
        P(None, "seq", None, "tp"),
        P(None, None, "tp"),
        P(None, ("tp", "seq"), None),
        P(None, ("tp", "seq")),
        P("tp", None),
        P(None, "seq", "tp"),
    )
    out_specs = (P(None, "seq", "tp"), P(None, "seq", None, "tp"), P(None, ("tp", "seq"), None))
    return jax.shard_map(local, mesh=mesh, in_specs=in_specs, out_specs=out_specs, check_vma=False)
```
